32 devices in a mesh: layer: 16 (over z, x, core), row: 2 (over y).
Axes of the slice: x: 2, y: 2, z: 4, core: 2. Of those that a mesh axis runs over, the one named last changes fastest.
Arguments:
- waves: bfloat16 [16, 3072, 512], P('layer', 'row'), may hold values from -6 to 6
- operators: bfloat16 [16, 4, 3072, 3072], P('layer', None, 'row'), may hold values from -0.0546875 to 0.0546875
- sources: bfloat16 [3072, 512], P('row'), may hold values from -6 to 6
- source_layer: int32 [128], replicated, may hold values from 0 to 15
Outputs:
- traces: bfloat16 [16, 3072, 512], P('layer', 'row')
The draws below stay inside these ranges and needn't reach their ends.
All inputs are finite; a program needn't handle non-finite values.
Results may differ from the reference program's by a relative error of at most 0.0057.
Values may be sent and summed in bfloat16 or wider, within the bound.
A program may use at most 128 MiB of HBM per device.

```python
import jax
import jax.numpy as jnp
from jax import lax

M = 3072
C = 128
TICKS = 3
LAYERS = 16


def touch_ends(result, stream_key, least, top_value):
    place = [jax.random.randint(jax.random.fold_in(stream_key, axis), (), 0, length) for axis, length in enumerate(result.shape)]
    widest = result.shape.index(max(result.shape))
    next_to = place[:widest] + [(place[widest] + 1) % result.shape[widest]] + place[widest + 1:]
    return result.at[tuple(place)].set(least).at[tuple(next_to)].set(top_value)


def steps_of(stream_key, shape, shards, low, top_value):
    factor_of = 1.0
    for position, blocks in shards:
        steps = jax.random.uniform(jax.random.fold_in(jax.random.fold_in(stream_key, 6), position), (blocks,), jnp.float32, low / len(shards), top_value / len(shards))
        factor_of = factor_of * jnp.repeat(jnp.exp(steps), shape[position] // blocks).reshape((-1,) + (1,) * (len(shape) - 1 - position))
    return factor_of


def bell_draw(own_key, shape, scale, limit, cuts=(), kind=jnp.bfloat16):
    array = scale * jax.random.normal(own_key, shape, jnp.float32)
    if cuts:
        array = array * steps_of(own_key, shape, cuts, -0.22, 0.18)
    return jnp.clip(array, -limit, limit).astype(kind)


def setup_inputs(seed: int = 0) -> dict:
    key_list = jax.random.split(jax.random.key(seed), 5)
    waves = bell_draw(key_list[0], (LAYERS, M, 4 * C), 1.0, 6.0, ((0, 16), (1, 2)))
    operators = bell_draw(key_list[1], (LAYERS, 4, M, M), (4 * M) ** -0.5, 0.0546875, ((0, 16), (2, 2)))
    sources = bell_draw(key_list[2], (M, 4 * C), 1.0, 6.0, ((0, 2),))
    source_layer = touch_ends(jax.random.randint(key_list[3], (C,), 0, LAYERS), jax.random.fold_in(key_list[3], 1), 0, LAYERS - 1).astype(jnp.int32)
    return dict(waves=waves, operators=operators, sources=sources, source_layer=source_layer)


def combine(real_prod, imag_prod, shot_count):
    real_part = real_prod[:, :shot_count] - imag_prod[:, shot_count:]
    imag_part = real_prod[:, shot_count:] + imag_prod[:, :shot_count]
    return jnp.concatenate([real_part, imag_part], axis=1)


def layer_tick(operator_block, wave_block, layer_id, sources, source_layer):
    full_rows = operator_block.shape[1]
    products = jnp.dot(operator_block.reshape(4 * full_rows, full_rows), wave_block, preferred_element_type=jnp.float32)
    products = products.reshape(4, full_rows, 4 * C)
    half = 2 * C
    down_out = combine(products[0][:, :half], products[1][:, :half], C) + combine(products[2][:, half:], products[3][:, half:], C)
    up_out = combine(products[0][:, half:], products[1][:, half:], C) + combine(products[2][:, :half], products[3][:, :half], C)
    shot_mask = jnp.tile((source_layer == layer_id).astype(jnp.float32), 4)
    source_term = sources.astype(jnp.float32) * shot_mask[None, :]
    down_out = (down_out + source_term[:, :half]).astype(jnp.bfloat16)
    up_out = (up_out + source_term[:, half:]).astype(jnp.bfloat16)
    return down_out, up_out


def reference(waves, operators, sources, source_layer):
    current = waves
    layer_ids = jnp.arange(LAYERS).astype(jnp.int32)
    for sweep_tick in range(TICKS):
        downs, ups = lax.map(lambda packed: layer_tick(packed[0], packed[1], packed[2], sources, source_layer), (operators, current, layer_ids))
        empty_rim = jnp.zeros((1, M, 2 * C), jnp.bfloat16)
        new_down = jnp.concatenate([empty_rim, downs[:-1]], axis=0)
        new_up = jnp.concatenate([ups[1:], empty_rim], axis=0)
        current = jnp.concatenate([new_down, new_up], axis=2)
    return current
```

```python
import functools
import math

import jax
import jax.numpy as jnp
from jax import lax
from jax.experimental import pallas as pl
from jax.experimental.pallas import tpu as pltpu
from jax.sharding import PartitionSpec as P

TICKS = 3
LAST = TICKS - 1
MESH = pl.DeviceIdType.MESH


def swap_halves(first, second):
    half = first.shape[1] // 2
    low = lax.broadcasted_iota(jnp.int32, first.shape, 1) < half
    return (
        jnp.where(low, first, pltpu.roll(second, half, 1)),
        jnp.where(low, pltpu.roll(first, half, 1), second),
    )


def even_quarter(shape):
    return jnp.bitwise_and(lax.broadcasted_iota(jnp.int32, shape, 1), shape[1] // 4) == 0


def swap_quarters(first, second):
    quarter = first.shape[1] // 4
    even = even_quarter(first.shape)
    return (
        jnp.where(even, first, pltpu.roll(second, quarter, 1)),
        jnp.where(even, pltpu.roll(first, 3 * quarter, 1), second),
    )


def turn(block):
    half = block.shape[1] // 2
    rolled = pltpu.roll(block, half, 1)
    return jnp.where(lax.broadcasted_iota(jnp.int32, block.shape, 1) < half, -rolled, rolled)


def exchange_quarters(block):
    quarter = block.shape[1] // 4
    return jnp.where(even_quarter(block.shape), pltpu.roll(block, 3 * quarter, 1), pltpu.roll(block, quarter, 1))


def kernel(
    layers, row_parts, chunk, big, deep, tall,
    waves, operators, sources, source_layer, final, final_sub,
    held, current, turned, total, outgoing, source_term, stage, sub, spun, total_sub, outgoing_sub,
    wave_sem, source_sem, load_sem, zero_sem, row_send, send_sem, recv_sem, final_sem,
    sub_send, sub_recv, last_send, last_recv,
):
    layer = lax.axis_index("layer")
    part = lax.axis_index("row")
    rows, lanes = outgoing.shape[2], outgoing.shape[3]
    depth = current.shape[3]
    chunks, deeps = rows // chunk, rows // deep
    pair = chunk // 2
    has_above, has_below = layer > 0, layer < layers - 1

    def piece(i, size=chunk, base=0):
        return pl.ds(pl.multiple_of(base + i * size, math.gcd(size, rows)), size)

    def load(i):
        span = piece(i, big)
        return pltpu.make_async_copy(operators.at[0, :, span, :], held.at[:, span, :], load_sem.at[i])

    def wave_load(i):
        return pltpu.make_async_copy(waves.at[0, piece(i), :], stage.at[piece(i), :], wave_sem.at[i])

    source_load = pltpu.make_async_copy(sources, stage, source_sem.at[0])
    for i in range(chunks):
        wave_load(i).start()

    barrier = pltpu.get_barrier_semaphore()
    for d in range(1, row_parts):
        pl.semaphore_signal(barrier, inc=1, device_id=(layer, lax.rem(part + d, row_parts)), device_id_type=MESH)
    for present, other in ((has_above, layer - 1), (has_below, layer + 1)):
        @pl.when(present)
        def _():
            pl.semaphore_signal(barrier, inc=1, device_id=(other, part), device_id_type=MESH)

    for i in range(rows // big):
        load(i).start()

    def packed(span):
        for way in range(2):
            at = 2 * way * lanes
            re = stage[span, at:at + lanes].astype(jnp.float32)
            im = stage[span, at + lanes:at + 2 * lanes].astype(jnp.float32)
            yield way, swap_halves(re, im)

    own_base = part * rows

    peers = row_parts - 1 + has_above.astype(jnp.int32) + has_below.astype(jnp.int32)
    pl.semaphore_wait(barrier, peers)

    def forward(tick, group, way, span):
        for d in range(1, row_parts):
            pltpu.make_async_remote_copy(
                src_ref=current.at[tick, group, way, span, :],
                dst_ref=current.at[tick, group, way, span, :],
                send_sem=row_send.at[tick, group, way, d - 1],
                recv_sem=recv_sem.at[tick, group, way, part],
                device_id=(layer, lax.rem(part + d, row_parts)),
                device_id_type=MESH,
            ).start()

    @pl.loop(0, chunks)
    def _(i):
        wave_load(i).wait()
        span = piece(i, chunk, own_base)
        for way, groups in packed(piece(i)):
            for group in range(2):
                current[0, group, way, span, :] = groups[group].astype(jnp.bfloat16)
        forward(0, 0, 0, span)
        forward(0, 0, 1, span)

    own = piece(0, rows, own_base)
    forward(0, 1, 0, own)
    forward(0, 1, 1, own)

    source_load.start()
    source_load.wait()
    mask = (source_layer[...] == layer).astype(jnp.float32)
    both = jnp.concatenate([mask, mask], 1)
    packed_mask = swap_halves(both[:, :lanes], both[:, lanes:])

    @pl.loop(0, chunks)
    def _(i):
        for way, groups in packed(piece(i)):
            for group in range(2):
                source_term[group, way, piece(i), :] = (groups[group] * packed_mask[group]).astype(jnp.bfloat16)

    def zero_final(way):
        empty = current.at[1, 0, way]
        yield pltpu.make_async_copy(empty.at[pl.ds(0, rows), :], final.at[way], zero_sem.at[way, 0])
        for q in range(2):
            yield pltpu.make_async_copy(empty.at[pl.ds(0, rows // 2), :], final_sub.at[q, way], zero_sem.at[way, 1 + q])

    for way, present in ((0, has_above), (1, has_below)):
        @pl.when(jnp.logical_not(present))
        def _():
            for group in range(2):
                for tick in range(1, TICKS):
                    @pl.loop(0, depth // chunk)
                    def _(i):
                        current[tick, group, way, piece(i), :] = jnp.zeros((chunk, lanes), jnp.bfloat16)
            for copy in zero_final(way):
                copy.start()

    def arrived(tick, group, way, p):
        ref = current.at[tick, group, way, piece(0, rows, p * rows), :]
        pltpu.make_async_copy(ref, ref, recv_sem.at[tick, group, way, p]).wait()

    def product(tick, group, span, inner):
        down, up = current[tick, group, 0, inner, :], current[tick, group, 1, inner, :]
        down_turned, up_turned = turned[0], turned[1]
        out = jnp.dot(held[0, span, inner], jnp.concatenate([down, up], 1), preferred_element_type=jnp.float32)
        out += jnp.dot(held[1, span, inner], jnp.concatenate([down_turned, up_turned], 1), preferred_element_type=jnp.float32)
        out += jnp.dot(held[2, span, inner], jnp.concatenate([up, down], 1), preferred_element_type=jnp.float32)
        out += jnp.dot(held[3, span, inner], jnp.concatenate([up_turned, down_turned], 1), preferred_element_type=jnp.float32)
        return out

    def part_of(d):
        p = lax.rem(part + d, row_parts)
        return p, pl.ds(pl.multiple_of(p * rows, 128), rows)

    def turn_part(tick, group, p):
        @pl.loop(0, chunks)
        def _(i):
            for way in range(2):
                block = current[tick, group, way, piece(i, chunk, p * rows), :].astype(jnp.float32)
                turned[way, piece(i), :] = turn(block).astype(jnp.bfloat16)

    def own_half(tick, group, first):
        p, inner = part_of(0)
        turn_part(tick, group, p)

        @pl.loop(0, rows // big)
        def _(i):
            @pl.when(first)
            def _():
                load(i).wait()
            total[piece(i, big), :] = product(tick, group, piece(i, big), inner)

    def other_half(tick, group, send):
        for d in range(1, row_parts):
            p, inner = part_of(d)
            for way, present in ((0, has_above), (1, has_below)):
                @pl.when(jnp.logical_or(tick == 0, present))
                def _():
                    arrived(tick, group, way, p)
            turn_part(tick, group, p)
            if d < row_parts - 1:
                @pl.loop(0, rows // big)
                def _(i):
                    span = piece(i, big)
                    total[span, :] += product(tick, group, span, inner)
                continue

            @pl.loop(0, chunks)
            def _(i):
                span = piece(i)
                out = product(tick, group, span, inner) + total[span, :]
                step = 2 * tick + group
                for way in range(2):
                    value = out[:, way * lanes:(way + 1) * lanes] + source_term[group, way, span, :].astype(jnp.float32)
                    outgoing[step, way, span, :] = value.astype(jnp.bfloat16)
                send(step, span, piece(i, chunk, own_base))

    ways = ((0, has_below, layer + 1), (1, has_above, layer - 1))

    def send_next(step, span, there):
        tick, group = step // 2, step % 2
        for way, present, other in ways:
            @pl.when(present)
            def _():
                pltpu.make_async_remote_copy(
                    src_ref=outgoing.at[step, way, span, :],
                    dst_ref=current.at[tick + 1, group, way, there, :],
                    send_sem=send_sem.at[step, way],
                    recv_sem=recv_sem.at[tick + 1, group, way, part],
                    device_id=(other, part),
                    device_id_type=MESH,
                ).start()

    def send_final(step, span, there):
        for way, present, other in ways:
            @pl.when(present)
            def _():
                pltpu.make_async_remote_copy(
                    src_ref=outgoing.at[step, way, span, :],
                    dst_ref=final.at[way, span, :],
                    send_sem=send_sem.at[step, way],
                    recv_sem=final_sem.at[way],
                    device_id=(other, part),
                    device_id_type=MESH,
                ).start()

    def take_next(step):
        tick, group = step // 2, step % 2
        for way, present in ((0, has_above), (1, has_below)):
            @pl.when(jnp.logical_and(present, step >= 2))
            def _():
                arrived(tick, group, way, part)
                forward(tick, group, way, own)

    def take_sub():
        for way, present in ((0, has_above), (1, has_below)):
            @pl.when(present)
            def _():
                arrived(LAST, 1, way, part)

        @pl.loop(0, chunks)
        def _(i):
            span = piece(i, chunk, own_base)
            down = current[LAST, 1, 0, span, :].astype(jnp.float32)
            up = current[LAST, 1, 1, span, :].astype(jnp.float32)
            for q, block in enumerate(swap_quarters(down, up)):
                sub[q, span, :] = block.astype(jnp.bfloat16)

        for q in range(2):
            for k in range(deeps):
                for d in range(1, row_parts):
                    span = piece(k, deep, own_base)
                    pltpu.make_async_remote_copy(
                        src_ref=sub.at[q, span, :],
                        dst_ref=sub.at[q, span, :],
                        send_sem=sub_send.at[q, d - 1],
                        recv_sem=sub_recv.at[q, k, part],
                        device_id=(layer, lax.rem(part + d, row_parts)),
                        device_id_type=MESH,
                    ).start()

    def own_sub():
        p, inner = part_of(0)
        turn_part(LAST, 1, p)

        @pl.loop(0, rows // big)
        def _(i):
            span = piece(i, big)
            out = product(LAST, 1, span, inner)
            sides = [
                out[:, way * lanes:(way + 1) * lanes] + source_term[1, way, span, :].astype(jnp.float32)
                for way in range(2)
            ]
            for q, block in enumerate(swap_quarters(*sides)):
                total_sub[q, span, :] = block

    def take_block(q, p, k):
        span = piece(k, deep, p * rows)
        ref = sub.at[q, span, :]
        pltpu.make_async_copy(ref, ref, sub_recv.at[q, k, p]).wait()
        block = sub[q, span, :].astype(jnp.float32)
        swapped = exchange_quarters(block)
        for n, value in enumerate((turn(block), swapped, turn(swapped))):
            spun[n] = value.astype(jnp.bfloat16)

    def product_sub(q, p, k, span):
        inner = pl.ds(pl.multiple_of(p * rows + k * deep, 128), deep)
        out = jnp.dot(held[0, span, inner], sub[q, inner, :], preferred_element_type=jnp.float32)
        for n in range(3):
            out += jnp.dot(held[1 + n, span, inner], spun[n], preferred_element_type=jnp.float32)
        return out + total_sub[q, span, :]

    def other_sub(q):
        for d in range(1, row_parts):
            p = lax.rem(part + d, row_parts)
            done = deeps if d < row_parts - 1 else deeps - 1

            if done:
                @pl.loop(0, done)
                def _(k):
                    take_block(q, p, k)

                    @pl.loop(0, rows // tall)
                    def _(i):
                        span = piece(i, tall)
                        total_sub[q, span, :] = product_sub(q, p, k, span)

        take_block(q, p, deeps - 1)

        @pl.loop(0, chunks)
        def _(i):
            out = product_sub(q, p, deeps - 1, piece(i))
            here = piece(i, pair)
            for (way, present, other), block in zip(ways, swap_quarters(out[:pair], out[pair:])):
                outgoing_sub[q, way, here, :] = block.astype(jnp.bfloat16)

                @pl.when(present)
                def _():
                    pltpu.make_async_remote_copy(
                        src_ref=outgoing_sub.at[q, way, here, :],
                        dst_ref=final_sub.at[q, way, here, :],
                        send_sem=last_send.at[q, way],
                        recv_sem=last_recv.at[q, way],
                        device_id=(other, part),
                        device_id_type=MESH,
                    ).start()

    @pl.loop(0, 2 * LAST)
    def _(step):
        tick, group = step // 2, step % 2
        own_half(tick, group, step == 0)
        take_next(step + 1)
        other_half(tick, group, send_next)

    own_half(LAST, 0, layer < 0)
    take_sub()
    own_sub()
    other_half(LAST, 0, send_final)
    for q in range(2):
        other_sub(q)

    def whole(ref, sem):
        pltpu.make_async_copy(ref, ref, sem).wait()

    for way, came, goes in ((0, has_above, has_below), (1, has_below, has_above)):
        def sent(tick, group):
            for d in range(1, row_parts):
                whole(current.at[tick, group, way, own, :], row_send.at[tick, group, way, d - 1])

        for group in range(2):
            sent(0, group)

        @pl.when(came)
        def _():
            for step in range(2, 2 * LAST + 1):
                sent(step // 2, step % 2)
            whole(final.at[way], final_sem.at[way])
            for q in range(2):
                whole(final_sub.at[q, way], last_recv.at[q, way])

        @pl.when(jnp.logical_not(came))
        def _():
            for copy in zero_final(way):
                copy.wait()

        @pl.when(goes)
        def _():
            for step in range(2 * LAST + 1):
                whole(outgoing.at[step, way], send_sem.at[step, way])
            for q in range(2):
                whole(outgoing_sub.at[q, way], last_send.at[q, way])

    for q in range(2):
        for d in range(1, row_parts):
            whole(sub.at[q, own, :], sub_send.at[q, d - 1])


def unpack(chunk, final, final_sub, result, first, second, natural, first_sem, second_sem, out_sem):
    rows, lanes = first.shape[1], first.shape[2]
    pair = chunk // 2
    chunks = rows // chunk

    def takes(i):
        full, half = pl.ds(i * chunk, chunk), pl.ds(i * pair, pair)
        return (
            pltpu.make_async_copy(final.at[:, full, :], first.at[:, full, :], first_sem.at[i]),
            pltpu.make_async_copy(final_sub.at[:, :, half, :], second.at[:, :, half, :], second_sem.at[i]),
        )

    def put(i):
        full = pl.ds(i * chunk, chunk)
        return pltpu.make_async_copy(natural.at[full, :], result.at[0, full, :], out_sem.at[i])

    for i in range(chunks):
        for copy in takes(i):
            copy.start()
    for i in range(chunks):
        for copy in takes(i):
            copy.wait()
        full, half = pl.ds(i * chunk, chunk), pl.ds(i * pair, pair)
        for way in range(2):
            a = first[way, full, :].astype(jnp.float32)
            b = jnp.concatenate(
                swap_quarters(second[0, way, half, :].astype(jnp.float32), second[1, way, half, :].astype(jnp.float32)), 0
            )
            for n, block in enumerate(swap_halves(a, b)):
                at = (2 * way + n) * lanes
                natural[full, at:at + lanes] = block.astype(jnp.bfloat16)
        put(i).start()
    for i in range(chunks):
        put(i).wait()


def per_device(waves, operators, sources, source_layer):
    layers, row_parts = lax.axis_size("layer"), lax.axis_size("row")
    rows, depth = operators.shape[2], operators.shape[3]
    lanes = waves.shape[2] // 4
    chunk, big, deep, tall = (math.gcd(rows, size) for size in (256, 512, 384, 768))
    chunks, steps = rows // chunk, 2 * LAST + 1
    peers = row_parts - 1
    anywhere = pl.BlockSpec(memory_space=pl.ANY)
    dma = pltpu.SemaphoreType.DMA
    final, final_sub = pl.pallas_call(
        functools.partial(kernel, layers, row_parts, chunk, big, deep, tall),
        out_shape=(
            jax.ShapeDtypeStruct((2, rows, lanes), jnp.bfloat16),
            jax.ShapeDtypeStruct((2, 2, rows // 2, lanes), jnp.bfloat16),
        ),
        in_specs=[anywhere, anywhere, anywhere, pl.BlockSpec(memory_space=pltpu.VMEM)],
        out_specs=(anywhere, anywhere),
        scratch_shapes=[
            pltpu.VMEM((4, rows, depth), jnp.bfloat16),
            pltpu.VMEM((TICKS, 2, 2, depth, lanes), jnp.bfloat16),
            pltpu.VMEM((2, rows, lanes), jnp.bfloat16),
            pltpu.VMEM((rows, 2 * lanes), jnp.float32),
            pltpu.VMEM((steps, 2, rows, lanes), jnp.bfloat16),
            pltpu.VMEM((2, 2, rows, lanes), jnp.bfloat16),
            pltpu.VMEM((rows, 4 * lanes), jnp.bfloat16),
            pltpu.VMEM((2, depth, lanes), jnp.bfloat16),
            pltpu.VMEM((3, deep, lanes), jnp.bfloat16),
            pltpu.VMEM((2, rows, lanes), jnp.float32),
            pltpu.VMEM((2, 2, rows // 2, lanes), jnp.bfloat16),
            dma((chunks,)),
            dma((1,)),
            dma((rows // big,)),
            dma((2, 3)),
            dma((TICKS, 2, 2, peers)),
            dma((steps, 2)),
            dma((TICKS, 2, 2, row_parts)),
            dma((2,)),
            dma((2, peers)),
            dma((2, rows // deep, row_parts)),
            dma((2, 2)),
            dma((2, 2)),
        ],
        compiler_params=pltpu.CompilerParams(
            collective_id=0, has_side_effects=True, vmem_limit_bytes=67043328
        ),
    )(waves, operators, sources, source_layer.reshape(1, lanes))
    return pl.pallas_call(
        functools.partial(unpack, chunk),
        out_shape=jax.ShapeDtypeStruct(waves.shape, jnp.bfloat16),
        in_specs=[anywhere, anywhere],
        out_specs=anywhere,
        scratch_shapes=[
            pltpu.VMEM(final.shape, jnp.bfloat16),
            pltpu.VMEM(final_sub.shape, jnp.bfloat16),
            pltpu.VMEM((rows, 4 * lanes), jnp.bfloat16),
            dma((chunks,)),
            dma((chunks,)),
            dma((chunks,)),
        ],
    )(final, final_sub)


def solution(mesh):
    return jax.shard_map(
        per_device,
        mesh=mesh,
        in_specs=(P("layer", "row", None), P("layer", None, "row", None), P("row", None), P()),
        out_specs=P("layer", "row", None),
        check_vma=False,
    )
```

```python
import functools
import math

import jax
import jax.numpy as jnp
from jax import lax
from jax.experimental import pallas as pl
from jax.experimental.pallas import tpu as pltpu
from jax.sharding import PartitionSpec as P

TICKS = 3
LAST = TICKS - 1
MESH = pl.DeviceIdType.MESH


def swap_halves(first, second):
    half = first.shape[1] // 2
    low = lax.broadcasted_iota(jnp.int32, first.shape, 1) < half
    return (
        jnp.where(low, first, pltpu.roll(second, half, 1)),
        jnp.where(low, pltpu.roll(first, half, 1), second),
    )


def even_quarter(shape):
    return jnp.bitwise_and(lax.broadcasted_iota(jnp.int32, shape, 1), shape[1] // 4) == 0


def swap_quarters(first, second):
    quarter = first.shape[1] // 4
    even = even_quarter(first.shape)
    return (
        jnp.where(even, first, pltpu.roll(second, quarter, 1)),
        jnp.where(even, pltpu.roll(first, 3 * quarter, 1), second),
    )


def turn(block):
    half = block.shape[1] // 2
    rolled = pltpu.roll(block, half, 1)
    return jnp.where(lax.broadcasted_iota(jnp.int32, block.shape, 1) < half, -rolled, rolled)


def exchange_quarters(block):
    quarter = block.shape[1] // 4
    return jnp.where(even_quarter(block.shape), pltpu.roll(block, 3 * quarter, 1), pltpu.roll(block, quarter, 1))


def kernel(
    layers, row_parts, fine, chunk, big, tall, slim, joint, deep, early,
    waves, operators, sources, source_layer, final, final_sub,
    held, current, turned, total, outgoing, source_term, stage, sub,
    wave_sem, source_sem, load_sem, zero_sem, row_send, send_sem, recv_sem, final_sem,
    block_recv, sub_send, sub_recv, last_send, last_recv, *relay_refs,
):
    layer = lax.axis_index("layer")
    part = lax.axis_index("row")
    rows, lanes = outgoing.shape[2], outgoing.shape[3]
    depth = current.shape[3]
    pieces, chunks = rows // fine, rows // chunk
    pair = slim // 2
    unit = math.gcd(math.gcd(fine, pair), deep)
    blocks = ([(joint, rows - joint)], [(start, deep) for start in range(joint, rows, deep)])
    left = rows - joint
    has_above, has_below = layer > 0, layer < layers - 1

    def piece(i, size=fine, base=0):
        return pl.ds(pl.multiple_of(base + i * size, unit), size)

    def load(i):
        span = piece(i, big)
        return pltpu.make_async_copy(operators.at[0, :, span, :], held.at[:, span, :], load_sem.at[i])

    def wave_load(i):
        return pltpu.make_async_copy(waves.at[0, piece(i), :], stage.at[piece(i), :], wave_sem.at[i])

    source_load = pltpu.make_async_copy(sources, stage, source_sem.at[0])
    for i in range(pieces):
        wave_load(i).start()

    barrier = pltpu.get_barrier_semaphore()
    for d in range(1, row_parts):
        pl.semaphore_signal(barrier, inc=1, device_id=(layer, lax.rem(part + d, row_parts)), device_id_type=MESH)
    for present, other in ((has_above, layer - 1), (has_below, layer + 1)):
        @pl.when(present)
        def _():
            pl.semaphore_signal(barrier, inc=1, device_id=(other, part), device_id_type=MESH)

    for i in range(rows // big):
        load(i).start()

    def packed(span):
        for way in range(2):
            at = 2 * way * lanes
            re = stage[span, at:at + lanes].astype(jnp.float32)
            im = stage[span, at + lanes:at + 2 * lanes].astype(jnp.float32)
            yield way, swap_halves(re, im)

    own_base = part * rows

    peers = row_parts - 1 + has_above.astype(jnp.int32) + has_below.astype(jnp.int32)
    pl.semaphore_wait(barrier, peers)

    def forward(tick, group, way, span, arrival=None):
        for d in range(1, row_parts):
            pltpu.make_async_remote_copy(
                src_ref=current.at[tick, group, way, span, :],
                dst_ref=current.at[tick, group, way, span, :],
                send_sem=row_send.at[tick, group, way, d - 1],
                recv_sem=recv_sem.at[tick, group, way, part] if arrival is None else arrival,
                device_id=(layer, lax.rem(part + d, row_parts)),
                device_id_type=MESH,
            ).start()

    @pl.loop(0, pieces)
    def _(i):
        wave_load(i).wait()
        span = piece(i, fine, own_base)
        for way, groups in packed(piece(i)):
            for group in range(2):
                current[0, group, way, span, :] = groups[group].astype(jnp.bfloat16)
        forward(0, 0, 0, span)
        forward(0, 0, 1, span)

    own = piece(0, rows, own_base)
    forward(0, 1, 0, own)
    forward(0, 1, 1, own)

    source_load.start()
    source_load.wait()
    mask = (source_layer[...] == layer).astype(jnp.float32)
    both = jnp.concatenate([mask, mask], 1)
    packed_mask = swap_halves(both[:, :lanes], both[:, lanes:])

    @pl.loop(0, pieces)
    def _(i):
        for way, groups in packed(piece(i)):
            for group in range(2):
                source_term[group, way, piece(i), :] = (groups[group] * packed_mask[group]).astype(jnp.bfloat16)

    def zero_final(way):
        empty = current.at[1, 0, way]
        yield pltpu.make_async_copy(empty.at[pl.ds(0, rows), :], final.at[way], zero_sem.at[way, 0])
        for q in range(2):
            yield pltpu.make_async_copy(empty.at[pl.ds(0, rows // 2), :], final_sub.at[q, way], zero_sem.at[way, 1 + q])

    for way, present in ((0, has_above), (1, has_below)):
        @pl.when(jnp.logical_not(present))
        def _():
            for group in range(2):
                for tick in range(1, TICKS):
                    @pl.loop(0, depth // fine)
                    def _(i):
                        current[tick, group, way, piece(i), :] = jnp.zeros((fine, lanes), jnp.bfloat16)
            for copy in zero_final(way):
                copy.start()

    def arrived(tick, group, way, p):
        ref = current.at[tick, group, way, piece(0, rows, p * rows), :]
        pltpu.make_async_copy(ref, ref, recv_sem.at[tick, group, way, p]).wait()

    def multiply(span, inner, columns):
        return jnp.dot(
            jnp.concatenate([held[m, span, inner] for m in range(4)], 1),
            jnp.concatenate(columns, 0),
            preferred_element_type=jnp.float32,
        )

    def product(tick, group, span, inner):
        down, up = current[tick, group, 0, inner, :], current[tick, group, 1, inner, :]
        down_turned, up_turned = turned[0, :inner.size, :], turned[1, :inner.size, :]
        columns = ((down, up), (down_turned, up_turned), (up, down), (up_turned, down_turned))
        return multiply(span, inner, [jnp.concatenate(pair_of, 1) for pair_of in columns])

    def part_of(d):
        p = lax.rem(part + d, row_parts)
        return p, pl.ds(pl.multiple_of(p * rows, 128), rows)

    def turn_part(tick, group, inner):
        size = math.gcd(inner.size, 768)

        @pl.loop(0, inner.size // size)
        def _(i):
            for way in range(2):
                block = current[tick, group, way, piece(i, size, inner.start), :].astype(jnp.float32)
                turned[way, piece(i, size), :] = turn(block).astype(jnp.bfloat16)

    ways = ((0, has_below, layer + 1), (1, has_above, layer - 1))

    def sender(way):
        return layer - 1 if way == 0 else layer + 1

    def crosses_early(step, way, sender):
        if not early:
            return jnp.bool_(False)
        rank = sender if way == 0 else layers - 1 - sender
        last = sum((rank == r).astype(jnp.int32) * count for r, count in early)
        return jnp.logical_and(step >= 0, step < last)

    def relay(step, i, into_last=False):
        if not early:
            return
        held_back, _, relay_send, relay_recv = relay_refs
        span = piece(i, big)
        for way, present, other in ways:
            @pl.when(crosses_early(step, way, layer))
            def _():
                ref = held_back.at[step, span, :]
                pltpu.make_async_copy(ref, ref, relay_recv.at[step, i]).wait()
                pltpu.make_async_remote_copy(
                    src_ref=ref,
                    dst_ref=current.at[step // 2 + 1, step % 2, way, piece(i, big, (1 - part) * rows), :],
                    send_sem=relay_send.at[step],
                    recv_sem=block_recv.at[way, i, 1 - part] if into_last else recv_sem.at[step // 2 + 1, step % 2, way, 1 - part],
                    device_id=(other, part),
                    device_id_type=MESH,
                ).start()

    def own_half(tick, group, relays=True):
        _, inner = part_of(0)
        turn_part(tick, group, inner)

        @pl.loop(0, rows // big)
        def _(i):
            step = 2 * tick + group

            @pl.when(step == 0)
            def _():
                load(i).wait()
            total[group, piece(i, big), :] = product(tick, group, piece(i, big), inner)
            if relays:
                relay(step - 2, i)

    def leave(tick, group, span, inner):
        out = product(tick, group, span, inner) + total[group, span, :]
        for way in range(2):
            value = out[:, way * lanes:(way + 1) * lanes] + source_term[group, way, span, :].astype(jnp.float32)
            if isinstance(tick, int) and tick == LAST:
                stage[span, way * lanes:(way + 1) * lanes] = value.astype(jnp.bfloat16)
            else:
                outgoing[2 * tick + group, way, span, :] = value.astype(jnp.bfloat16)

    def other_half(tick, group):
        for d in range(1, row_parts):
            p, inner = part_of(d)
            for way, present in ((0, has_above), (1, has_below)):
                @pl.when(jnp.logical_or(tick == 0, present))
                def _():
                    arrived(tick, group, way, p)
            turn_part(tick, group, inner)
            if d < row_parts - 1:
                @pl.loop(0, rows // big)
                def _(i):
                    span = piece(i, big)
                    total[group, span, :] += product(tick, group, span, inner)
                continue

            @pl.loop(0, chunks)
            def _(i):
                span = piece(i, chunk)
                leave(tick, group, span, inner)
                send_next(2 * tick + group, span, piece(i, chunk, own_base), i)

    def send_next(step, span, there, i):
        tick, group = step // 2, step % 2
        for way, present, other in ways:
            @pl.when(present)
            def _():
                pltpu.make_async_remote_copy(
                    src_ref=outgoing.at[step, way, span, :],
                    dst_ref=current.at[tick + 1, group, way, there, :],
                    send_sem=send_sem.at[step, way],
                    recv_sem=recv_sem.at[tick + 1, group, way, part],
                    device_id=(other, part),
                    device_id_type=MESH,
                ).start()

            if early:
                held_back, early_send, _, relay_recv = relay_refs

                @pl.when(crosses_early(step, way, layer))
                def _():
                    pltpu.make_async_remote_copy(
                        src_ref=outgoing.at[step, way, span, :],
                        dst_ref=held_back.at[step, span, :],
                        send_sem=early_send.at[step],
                        recv_sem=relay_recv.at[step, i // (big // chunk)],
                        device_id=(layer, 1 - part),
                        device_id_type=MESH,
                    ).start()

    def send_final(step, span):
        for way, present, other in ways:
            @pl.when(present)
            def _():
                pltpu.make_async_remote_copy(
                    src_ref=stage.at[span, way * lanes:(way + 1) * lanes],
                    dst_ref=final.at[way, span, :],
                    send_sem=send_sem.at[step, way],
                    recv_sem=final_sem.at[way],
                    device_id=(other, part),
                    device_id_type=MESH,
                ).start()

    def take_next(step):
        tick, group = step // 2, step % 2
        for way, present in ((0, has_above), (1, has_below)):
            @pl.when(jnp.logical_and(present, step >= 2))
            def _():
                arrived(tick, group, way, part)

                @pl.when(jnp.logical_not(crosses_early(step - 2, way, sender(way))))
                def _():
                    forward(tick, group, way, own)

    def take_last():
        for way, present in ((0, has_above), (1, has_below)):
            @pl.when(present)
            def _():
                arrived(LAST, 0, way, part)

                @pl.when(jnp.logical_not(crosses_early(2 * LAST - 2, way, sender(way))))
                def _():
                    for k in range(rows // big):
                        forward(LAST, 0, way, piece(k, big, own_base), block_recv.at[way, k, part])

    def other_last(pairs):
        for d, k in pairs:
            p = lax.rem(part + d, row_parts)
            inner = piece(k, big, p * rows)
            for way, present in ((0, has_above), (1, has_below)):
                @pl.when(present)
                def _():
                    ref = current.at[LAST, 0, way, inner, :]
                    pltpu.make_async_copy(ref, ref, block_recv.at[way, k, p]).wait()
            turn_part(LAST, 0, inner)
            final_block = d == row_parts - 1 and k == rows // big - 1

            for i in range(rows // tall):
                span = piece(i, tall)
                if final_block:
                    leave(LAST, 0, span, inner)
                    send_final(2 * LAST, span)
                else:
                    total[0, span, :] += product(LAST, 0, span, inner)

    def take_sub():
        for way, present in ((0, has_above), (1, has_below)):
            @pl.when(present)
            def _():
                arrived(LAST, 1, way, part)
                forward(LAST, 1, way, piece(0, joint, own_base))

        @pl.loop(0, (rows - joint) // deep)
        def _(i):
            span = piece(i, deep, own_base + joint)
            down = current[LAST, 1, 0, span, :].astype(jnp.float32)
            up = current[LAST, 1, 1, span, :].astype(jnp.float32)
            for q, block in enumerate(swap_quarters(down, up)):
                sub[q, span, :] = block.astype(jnp.bfloat16)

        for q in range(2):
            for k, (start, size) in enumerate(blocks[q]):
                for d in range(1, row_parts):
                    span = pl.ds(pl.multiple_of(own_base + start, 128), size)
                    pltpu.make_async_remote_copy(
                        src_ref=sub.at[q, span, :],
                        dst_ref=sub.at[q, span, :],
                        send_sem=sub_send.at[q, d - 1],
                        recv_sem=sub_recv.at[q, k, part],
                        device_id=(layer, lax.rem(part + d, row_parts)),
                        device_id_type=MESH,
                    ).start()

    def own_sub():
        _, inner = part_of(0)
        turn_part(LAST, 1, inner)

        @pl.loop(0, rows // big)
        def _(i):
            span = piece(i, big)
            out = product(LAST, 1, span, inner)
            sides = [
                out[:, way * lanes:(way + 1) * lanes] + source_term[1, way, span, :].astype(jnp.float32)
                for way in range(2)
            ]
            for q, block in enumerate(swap_quarters(*sides)):
                total[1, span, q * lanes:(q + 1) * lanes] = block

    def joint_sub():
        for d in range(1, row_parts):
            p = lax.rem(part + d, row_parts)
            inner = piece(0, joint, p * rows)
            for way, present in ((0, has_above), (1, has_below)):
                @pl.when(present)
                def _():
                    ref = current.at[LAST, 1, way, inner, :]
                    pltpu.make_async_copy(ref, ref, recv_sem.at[LAST, 1, way, p]).wait()
            turn_part(LAST, 1, inner)

            for i in range(rows // tall):
                span = piece(i, tall)
                out = product(LAST, 1, span, inner)
                for q, block in enumerate(swap_quarters(out[:, :lanes], out[:, lanes:])):
                    total[1, span, q * lanes:(q + 1) * lanes] += block

    def other_sub(q):
        for d in range(1, row_parts):
            p = lax.rem(part + d, row_parts)
            for k, (start, size) in enumerate(blocks[q]):
                inner = pl.ds(pl.multiple_of(p * rows + start, 128), size)
                ref = sub.at[q, inner, :]
                pltpu.make_async_copy(ref, ref, sub_recv.at[q, k, p]).wait()

                @pl.loop(0, size // deep)
                def _(i):
                    block = sub[q, piece(i, deep, p * rows + start), :].astype(jnp.float32)
                    swapped = exchange_quarters(block)
                    for n, value in enumerate((turn(block), swapped, turn(swapped))):
                        turned[n // 2, piece(i, deep, n % 2 * left), :] = value.astype(jnp.bfloat16)

                def product_sub(span):
                    columns = [sub[q, inner, :]] + [turned[n // 2, pl.ds(n % 2 * left, size), :] for n in range(3)]
                    return multiply(span, inner, columns) + total[1, span, q * lanes:(q + 1) * lanes]

                if d < row_parts - 1 or k < len(blocks[q]) - 1:
                    for i in range(rows // tall):
                        span = piece(i, tall)
                        total[1, span, q * lanes:(q + 1) * lanes] = product_sub(span)
                    continue

                for i in range(rows // slim):
                    out = product_sub(piece(i, slim))
                    here = piece(i, pair)
                    for (way, present, other), block in zip(ways, swap_quarters(out[:pair], out[pair:])):
                        ours, at = piece(i, pair, q * (rows // 2)), (2 + way) * lanes
                        stage[ours, at:at + lanes] = block.astype(jnp.bfloat16)

                        @pl.when(present)
                        def _():
                            pltpu.make_async_remote_copy(
                                src_ref=stage.at[ours, at:at + lanes],
                                dst_ref=final_sub.at[q, way, here, :],
                                send_sem=last_send.at[q, way],
                                recv_sem=last_recv.at[q, way],
                                device_id=(other, part),
                                device_id_type=MESH,
                            ).start()

    @pl.loop(0, 2 * LAST - 1)
    def _(step):
        tick, group = step // 2, step % 2
        own_half(tick, group)
        take_next(step + 1)
        other_half(tick, group)

    own_half(LAST - 1, 1)
    take_last()
    own_half(LAST, 0, False)
    other_half(LAST - 1, 1)
    pairs = [(d, k) for d in range(1, row_parts) for k in range(rows // big)]
    ahead = max(rows // big - 1, 0)
    for i in range(rows // big):
        relay(2 * LAST - 2, i, True)
    other_last(pairs[:1])
    take_sub()
    other_last(pairs[1:ahead])
    own_sub()
    other_last(pairs[ahead:])
    joint_sub()
    for q in range(2):
        other_sub(q)

    def whole(ref, sem):
        pltpu.make_async_copy(ref, ref, sem).wait()

    for way, came, goes in ((0, has_above, has_below), (1, has_below, has_above)):
        def sent(tick, group):
            for d in range(1, row_parts):
                whole(current.at[tick, group, way, own, :], row_send.at[tick, group, way, d - 1])

        for group in range(2):
            sent(0, group)

        @pl.when(came)
        def _():
            for step in range(2, 2 * LAST + 1):
                @pl.when(jnp.logical_not(crosses_early(step - 2, way, sender(way))))
                def _():
                    sent(step // 2, step % 2)
            if joint:
                for d in range(1, row_parts):
                    whole(current.at[LAST, 1, way, piece(0, joint, own_base), :], row_send.at[LAST, 1, way, d - 1])
            whole(final.at[way], final_sem.at[way])
            for q in range(2):
                whole(final_sub.at[q, way], last_recv.at[q, way])

        @pl.when(jnp.logical_not(came))
        def _():
            for copy in zero_final(way):
                copy.wait()

        @pl.when(goes)
        def _():
            for step in range(2 * LAST + 1):
                whole(outgoing.at[0, way], send_sem.at[step, way])
            for q in range(2):
                whole(outgoing.at[0, way, pl.ds(0, rows // 2), :], last_send.at[q, way])

        if early:
            for step in range(2 * LAST - 1):
                @pl.when(crosses_early(step, way, layer))
                def _():
                    for sem in relay_refs[1:3]:
                        whole(outgoing.at[step, way], sem.at[step])

    for q in range(2):
        for d in range(1, row_parts):
            whole(sub.at[q, piece(0, rows - joint, own_base + joint), :], sub_send.at[q, d - 1])


def unpack(chunk, slim, final, final_sub, result, first, second, natural, first_sem, second_sem, out_sem):
    rows, lanes = first.shape[1], first.shape[2]
    pair = chunk // 2
    chunks = rows // chunk

    def takes(i):
        full, half = pl.ds(i * chunk, chunk), pl.ds(i * pair, pair)
        return (
            pltpu.make_async_copy(final.at[:, full, :], first.at[:, full, :], first_sem.at[i]),
            pltpu.make_async_copy(final_sub.at[:, :, half, :], second.at[:, :, half, :], second_sem.at[i]),
        )

    def put(i):
        full = pl.ds(i * chunk, chunk)
        return pltpu.make_async_copy(natural.at[full, :], result.at[0, full, :], out_sem.at[i])

    for i in range(chunks):
        for copy in takes(i):
            copy.start()
    for i in range(chunks):
        for copy in takes(i):
            copy.wait()
        full, half = pl.ds(i * chunk, chunk), pl.ds(i * pair, pair)
        for way in range(2):
            a = first[way, full, :].astype(jnp.float32)
            parts = []
            for j in range(chunk // slim):
                short = pl.ds(i * pair + j * (slim // 2), slim // 2)
                parts += swap_quarters(*(second[q, way, short, :].astype(jnp.float32) for q in range(2)))
            b = jnp.concatenate(parts, 0)
            for n, block in enumerate(swap_halves(a, b)):
                at = (2 * way + n) * lanes
                natural[full, at:at + lanes] = block.astype(jnp.bfloat16)
        put(i).start()
    for i in range(chunks):
        put(i).wait()


def level(layers):
    chips = layers // 2
    counts = [(2 * i + 1, min(2 * LAST - 1, 4 - 8 * (i + 1) // chips)) for i in range(chips // 2 - 1)]
    return tuple((rank, count) for rank, count in counts if count > 0)


def per_device(waves, operators, sources, source_layer):
    layers, row_parts = lax.axis_size("layer"), lax.axis_size("row")
    rows, depth = operators.shape[2], operators.shape[3]
    lanes = waves.shape[2] // 4
    fine, chunk, big, tall, slim, deep, broad = (math.gcd(rows, size) for size in (256, 512, 512, 256, 256, 384, 512))
    deep = deep if deep < rows else math.gcd(rows, 128)
    joint = rows // deep // 2 * deep
    early = ()
    pieces, steps = rows // broad, 2 * LAST + 1
    peers = row_parts - 1
    anywhere = pl.BlockSpec(memory_space=pl.ANY)
    dma = pltpu.SemaphoreType.DMA
    relays = 2 * LAST - 1
    relay_shapes = [
        pltpu.VMEM((relays, rows, lanes), jnp.bfloat16),
        dma((relays,)),
        dma((relays,)),
        dma((relays, rows // big)),
    ] if early else []
    final, final_sub = pl.pallas_call(
        functools.partial(kernel, layers, row_parts, fine, chunk, big, tall, slim, joint, deep, early),
        out_shape=(
            jax.ShapeDtypeStruct((2, rows, lanes), jnp.bfloat16),
            jax.ShapeDtypeStruct((2, 2, rows // 2, lanes), jnp.bfloat16),
        ),
        in_specs=[anywhere, anywhere, anywhere, pl.BlockSpec(memory_space=pltpu.VMEM)],
        out_specs=(anywhere, anywhere),
        scratch_shapes=[
            pltpu.VMEM((4, rows, depth), jnp.bfloat16),
            pltpu.VMEM((TICKS, 2, 2, depth, lanes), jnp.bfloat16),
            pltpu.VMEM((2, max(rows, 2 * (rows - joint)), lanes), jnp.bfloat16),
            pltpu.VMEM((2, rows, 2 * lanes), jnp.float32),
            pltpu.VMEM((steps - 1, 2, rows, lanes), jnp.bfloat16),
            pltpu.VMEM((2, 2, rows, lanes), jnp.bfloat16),
            pltpu.VMEM((rows, 4 * lanes), jnp.bfloat16),
            pltpu.VMEM((2, depth, lanes), jnp.bfloat16),
            dma((rows // fine,)),
            dma((1,)),
            dma((rows // big,)),
            dma((2, 3)),
            dma((TICKS, 2, 2, peers)),
            dma((steps, 2)),
            dma((TICKS, 2, 2, row_parts)),
            dma((2,)),
            dma((2, rows // big, row_parts)),
            dma((2, peers)),
            dma((2, (rows - joint) // deep, row_parts)),
            dma((2, 2)),
            dma((2, 2)),
            *relay_shapes,
        ],
        compiler_params=pltpu.CompilerParams(
            collective_id=0, has_side_effects=True, vmem_limit_bytes=67043328
        ),
    )(waves, operators, sources, source_layer.reshape(1, lanes))
    return pl.pallas_call(
        functools.partial(unpack, broad, slim),
        out_shape=jax.ShapeDtypeStruct(waves.shape, jnp.bfloat16),
        in_specs=[anywhere, anywhere],
        out_specs=anywhere,
        scratch_shapes=[
            pltpu.VMEM(final.shape, jnp.bfloat16),
            pltpu.VMEM(final_sub.shape, jnp.bfloat16),
            pltpu.VMEM((rows, 4 * lanes), jnp.bfloat16),
            dma((pieces,)),
            dma((pieces,)),
            dma((pieces,)),
        ],
    )(final, final_sub)


def solution(mesh):
    return jax.shard_map(
        per_device,
        mesh=mesh,
        in_specs=(P("layer", "row", None), P("layer", None, "row", None), P("row", None), P()),
        out_specs=P("layer", "row", None),
        check_vma=False,
    )
```

```python
import functools
import math

import jax
import jax.numpy as jnp
from jax import lax
from jax.experimental import pallas as pl
from jax.experimental.pallas import tpu as pltpu
from jax.sharding import PartitionSpec as P

TICKS = 3
LAST = TICKS - 1
MESH = pl.DeviceIdType.MESH


def swap_halves(first, second):
    half = first.shape[1] // 2
    low = lax.broadcasted_iota(jnp.int32, first.shape, 1) < half
    return (
        jnp.where(low, first, pltpu.roll(second, half, 1)),
        jnp.where(low, pltpu.roll(first, half, 1), second),
    )


def even_quarter(shape):
    return jnp.bitwise_and(lax.broadcasted_iota(jnp.int32, shape, 1), shape[1] // 4) == 0


def swap_quarters(first, second):
    quarter = first.shape[1] // 4
    even = even_quarter(first.shape)
    return (
        jnp.where(even, first, pltpu.roll(second, quarter, 1)),
        jnp.where(even, pltpu.roll(first, 3 * quarter, 1), second),
    )


def turn(block):
    half = block.shape[1] // 2
    rolled = pltpu.roll(block, half, 1)
    return jnp.where(lax.broadcasted_iota(jnp.int32, block.shape, 1) < half, -rolled, rolled)


def exchange_quarters(block):
    quarter = block.shape[1] // 4
    return jnp.where(even_quarter(block.shape), pltpu.roll(block, 3 * quarter, 1), pltpu.roll(block, quarter, 1))


def kernel(
    layers, row_parts, fine, chunk, big, tall, slim, joint, deep, early,
    waves, operators, sources, source_layer, final, final_sub,
    held, current, turned, total, outgoing, source_term, stage, sub,
    wave_sem, source_sem, load_sem, zero_sem, row_send, send_sem, recv_sem, final_sem,
    block_recv, sub_send, sub_recv, last_send, last_recv, *relay_refs,
):
    layer = lax.axis_index("layer")
    part = lax.axis_index("row")
    rows, lanes = outgoing.shape[2], outgoing.shape[3]
    depth = current.shape[3]
    pieces, chunks = rows // fine, rows // chunk
    pair = slim // 2
    unit = math.gcd(math.gcd(fine, pair), deep)
    blocks = [[(start, deep) for start in range(joint, rows, deep)]] * 2
    left = rows - joint
    has_above, has_below = layer > 0, layer < layers - 1

    def piece(i, size=fine, base=0):
        return pl.ds(pl.multiple_of(base + i * size, unit), size)

    def load(i):
        span = piece(i, big)
        return pltpu.make_async_copy(operators.at[0, :, span, :], held.at[:, span, :], load_sem.at[i])

    def wave_load(i):
        return pltpu.make_async_copy(waves.at[0, piece(i), :], stage.at[piece(i), :], wave_sem.at[i])

    source_load = pltpu.make_async_copy(sources, stage, source_sem.at[0])
    for i in range(pieces):
        wave_load(i).start()

    barrier = pltpu.get_barrier_semaphore()
    for d in range(1, row_parts):
        pl.semaphore_signal(barrier, inc=1, device_id=(layer, lax.rem(part + d, row_parts)), device_id_type=MESH)
    for present, other in ((has_above, layer - 1), (has_below, layer + 1)):
        @pl.when(present)
        def _():
            pl.semaphore_signal(barrier, inc=1, device_id=(other, part), device_id_type=MESH)

    def packed(span):
        for way in range(2):
            at = 2 * way * lanes
            re = stage[span, at:at + lanes].astype(jnp.float32)
            im = stage[span, at + lanes:at + 2 * lanes].astype(jnp.float32)
            yield way, swap_halves(re, im)

    own_base = part * rows

    peers = row_parts - 1 + has_above.astype(jnp.int32) + has_below.astype(jnp.int32)
    pl.semaphore_wait(barrier, peers)

    def forward(tick, group, way, span, arrival=None):
        for d in range(1, row_parts):
            pltpu.make_async_remote_copy(
                src_ref=current.at[tick, group, way, span, :],
                dst_ref=current.at[tick, group, way, span, :],
                send_sem=row_send.at[tick, group, way, d - 1],
                recv_sem=recv_sem.at[tick, group, way, part] if arrival is None else arrival,
                device_id=(layer, lax.rem(part + d, row_parts)),
                device_id_type=MESH,
            ).start()

    @pl.loop(0, pieces)
    def _(i):
        wave_load(i).wait()
        span = piece(i, fine, own_base)
        for way, groups in packed(piece(i)):
            for group in range(2):
                current[0, group, way, span, :] = groups[group].astype(jnp.bfloat16)
        forward(0, 0, 0, span)
        forward(0, 0, 1, span)

    for i in range(rows // big):
        load(i).start()

    own = piece(0, rows, own_base)
    forward(0, 1, 0, own)
    forward(0, 1, 1, own)

    source_load.start()
    source_load.wait()
    mask = (source_layer[...] == layer).astype(jnp.float32)
    both = jnp.concatenate([mask, mask], 1)
    packed_mask = swap_halves(both[:, :lanes], both[:, lanes:])

    @pl.loop(0, pieces)
    def _(i):
        for way, groups in packed(piece(i)):
            for group in range(2):
                source_term[group, way, piece(i), :] = (groups[group] * packed_mask[group]).astype(jnp.bfloat16)

    def zero_final(way):
        empty = current.at[1, 0, way]
        yield pltpu.make_async_copy(empty.at[pl.ds(0, rows), :], final.at[way], zero_sem.at[way, 0])
        for q in range(2):
            yield pltpu.make_async_copy(empty.at[pl.ds(0, rows // 2), :], final_sub.at[q, way], zero_sem.at[way, 1 + q])

    for way, present in ((0, has_above), (1, has_below)):
        @pl.when(jnp.logical_not(present))
        def _():
            for group in range(2):
                for tick in range(1, TICKS):
                    @pl.loop(0, depth // fine)
                    def _(i):
                        current[tick, group, way, piece(i), :] = jnp.zeros((fine, lanes), jnp.bfloat16)
            for copy in zero_final(way):
                copy.start()

    def arrived(tick, group, way, p):
        ref = current.at[tick, group, way, piece(0, rows, p * rows), :]
        pltpu.make_async_copy(ref, ref, recv_sem.at[tick, group, way, p]).wait()

    def multiply(span, inner, columns):
        return jnp.dot(
            jnp.concatenate([held[m, span, inner] for m in range(4)], 1),
            jnp.concatenate(columns, 0),
            preferred_element_type=jnp.float32,
        )

    def product(tick, group, span, inner):
        down, up = current[tick, group, 0, inner, :], current[tick, group, 1, inner, :]
        down_turned, up_turned = turned[0, :inner.size, :], turned[1, :inner.size, :]
        columns = ((down, up), (down_turned, up_turned), (up, down), (up_turned, down_turned))
        return multiply(span, inner, [jnp.concatenate(pair_of, 1) for pair_of in columns])

    def part_of(d):
        p = lax.rem(part + d, row_parts)
        return p, pl.ds(pl.multiple_of(p * rows, 128), rows)

    def turn_part(tick, group, inner):
        size = math.gcd(inner.size, 768)

        @pl.loop(0, inner.size // size)
        def _(i):
            for way in range(2):
                block = current[tick, group, way, piece(i, size, inner.start), :].astype(jnp.float32)
                turned[way, piece(i, size), :] = turn(block).astype(jnp.bfloat16)

    ways = ((0, has_below, layer + 1), (1, has_above, layer - 1))

    def sender(way):
        return layer - 1 if way == 0 else layer + 1

    def crosses_early(step, way, sender):
        if not early:
            return jnp.bool_(False)
        rank = sender if way == 0 else layers - 1 - sender
        last = sum((rank == r).astype(jnp.int32) * count for r, count in early)
        return jnp.logical_and(step >= 0, step < last)

    def relay(step, i, into_last=False):
        if not early:
            return
        held_back, _, relay_send, relay_recv = relay_refs
        span = piece(i, big)
        for way, present, other in ways:
            @pl.when(crosses_early(step, way, layer))
            def _():
                ref = held_back.at[step, span, :]
                pltpu.make_async_copy(ref, ref, relay_recv.at[step, i]).wait()
                pltpu.make_async_remote_copy(
                    src_ref=ref,
                    dst_ref=current.at[step // 2 + 1, step % 2, way, piece(i, big, (1 - part) * rows), :],
                    send_sem=relay_send.at[step],
                    recv_sem=block_recv.at[way, i, 1 - part] if into_last else recv_sem.at[step // 2 + 1, step % 2, way, 1 - part],
                    device_id=(other, part),
                    device_id_type=MESH,
                ).start()

    def own_half(tick, group, relays=True):
        _, inner = part_of(0)
        turn_part(tick, group, inner)

        @pl.loop(0, rows // big)
        def _(i):
            step = 2 * tick + group

            @pl.when(step == 0)
            def _():
                load(i).wait()
            total[group, piece(i, big), :] = product(tick, group, piece(i, big), inner)
            if relays:
                relay(step - 2, i)

    def leave(tick, group, span, inner):
        out = product(tick, group, span, inner) + total[group, span, :]
        for way in range(2):
            value = out[:, way * lanes:(way + 1) * lanes] + source_term[group, way, span, :].astype(jnp.float32)
            if isinstance(tick, int) and tick == LAST:
                stage[span, way * lanes:(way + 1) * lanes] = value.astype(jnp.bfloat16)
            else:
                outgoing[2 * tick + group, way, span, :] = value.astype(jnp.bfloat16)

    def other_half(tick, group):
        for d in range(1, row_parts):
            p, inner = part_of(d)
            for way, present in ((0, has_above), (1, has_below)):
                @pl.when(jnp.logical_or(tick == 0, present))
                def _():
                    arrived(tick, group, way, p)
            turn_part(tick, group, inner)
            if d < row_parts - 1:
                @pl.loop(0, rows // big)
                def _(i):
                    span = piece(i, big)
                    total[group, span, :] += product(tick, group, span, inner)
                continue

            @pl.loop(0, chunks)
            def _(i):
                span = piece(i, chunk)
                leave(tick, group, span, inner)
                send_next(2 * tick + group, span, piece(i, chunk, own_base), i)

    def send_next(step, span, there, i):
        tick, group = step // 2, step % 2
        for way, present, other in ways:
            @pl.when(present)
            def _():
                pltpu.make_async_remote_copy(
                    src_ref=outgoing.at[step, way, span, :],
                    dst_ref=current.at[tick + 1, group, way, there, :],
                    send_sem=send_sem.at[step, way],
                    recv_sem=recv_sem.at[tick + 1, group, way, part],
                    device_id=(other, part),
                    device_id_type=MESH,
                ).start()

            if early:
                held_back, early_send, _, relay_recv = relay_refs

                @pl.when(crosses_early(step, way, layer))
                def _():
                    pltpu.make_async_remote_copy(
                        src_ref=outgoing.at[step, way, span, :],
                        dst_ref=held_back.at[step, span, :],
                        send_sem=early_send.at[step],
                        recv_sem=relay_recv.at[step, i // (big // chunk)],
                        device_id=(layer, 1 - part),
                        device_id_type=MESH,
                    ).start()

    def send_final(step, span):
        for way, present, other in ways:
            @pl.when(present)
            def _():
                pltpu.make_async_remote_copy(
                    src_ref=stage.at[span, way * lanes:(way + 1) * lanes],
                    dst_ref=final.at[way, span, :],
                    send_sem=send_sem.at[step, way],
                    recv_sem=final_sem.at[way],
                    device_id=(other, part),
                    device_id_type=MESH,
                ).start()

    def take_next(step):
        tick, group = step // 2, step % 2
        for way, present in ((0, has_above), (1, has_below)):
            @pl.when(jnp.logical_and(present, step >= 2))
            def _():
                arrived(tick, group, way, part)

                @pl.when(jnp.logical_not(crosses_early(step - 2, way, sender(way))))
                def _():
                    forward(tick, group, way, own)

    def take_last():
        for way, present in ((0, has_above), (1, has_below)):
            @pl.when(present)
            def _():
                arrived(LAST, 0, way, part)

                @pl.when(jnp.logical_not(crosses_early(2 * LAST - 2, way, sender(way))))
                def _():
                    for k in range(rows // big):
                        forward(LAST, 0, way, piece(k, big, own_base), block_recv.at[way, k, part])

    def other_last(pairs):
        for d, k in pairs:
            p = lax.rem(part + d, row_parts)
            inner = piece(k, big, p * rows)
            for way, present in ((0, has_above), (1, has_below)):
                @pl.when(present)
                def _():
                    ref = current.at[LAST, 0, way, inner, :]
                    pltpu.make_async_copy(ref, ref, block_recv.at[way, k, p]).wait()
            turn_part(LAST, 0, inner)
            final_block = d == row_parts - 1 and k == rows // big - 1

            for i in range(rows // tall):
                span = piece(i, tall)
                if final_block:
                    leave(LAST, 0, span, inner)
                    send_final(2 * LAST, span)
                else:
                    total[0, span, :] += product(LAST, 0, span, inner)

    def take_sub():
        for way, present in ((0, has_above), (1, has_below)):
            @pl.when(present)
            def _():
                arrived(LAST, 1, way, part)
                forward(LAST, 1, way, piece(0, joint, own_base))

        @pl.loop(0, (rows - joint) // deep)
        def _(i):
            span = piece(i, deep, own_base + joint)
            down = current[LAST, 1, 0, span, :].astype(jnp.float32)
            up = current[LAST, 1, 1, span, :].astype(jnp.float32)
            for q, block in enumerate(swap_quarters(down, up)):
                sub[q, span, :] = block.astype(jnp.bfloat16)

        for q in range(2):
            for k, (start, size) in enumerate(blocks[q]):
                for d in range(1, row_parts):
                    span = pl.ds(pl.multiple_of(own_base + start, 128), size)
                    pltpu.make_async_remote_copy(
                        src_ref=sub.at[q, span, :],
                        dst_ref=sub.at[q, span, :],
                        send_sem=sub_send.at[q, d - 1],
                        recv_sem=sub_recv.at[q, k, part],
                        device_id=(layer, lax.rem(part + d, row_parts)),
                        device_id_type=MESH,
                    ).start()

    def own_sub():
        _, inner = part_of(0)
        turn_part(LAST, 1, inner)

        @pl.loop(0, rows // big)
        def _(i):
            span = piece(i, big)
            out = product(LAST, 1, span, inner)
            sides = [
                out[:, way * lanes:(way + 1) * lanes] + source_term[1, way, span, :].astype(jnp.float32)
                for way in range(2)
            ]
            for q, block in enumerate(swap_quarters(*sides)):
                total[1, span, q * lanes:(q + 1) * lanes] = block

    def joint_sub():
        for d in range(1, row_parts):
            p = lax.rem(part + d, row_parts)
            inner = piece(0, joint, p * rows)
            for way, present in ((0, has_above), (1, has_below)):
                @pl.when(present)
                def _():
                    ref = current.at[LAST, 1, way, inner, :]
                    pltpu.make_async_copy(ref, ref, recv_sem.at[LAST, 1, way, p]).wait()
            turn_part(LAST, 1, inner)

            for i in range(rows // tall):
                span = piece(i, tall)
                out = product(LAST, 1, span, inner)
                for q, block in enumerate(swap_quarters(out[:, :lanes], out[:, lanes:])):
                    total[1, span, q * lanes:(q + 1) * lanes] += block

    def other_sub(q):
        for d in range(1, row_parts):
            p = lax.rem(part + d, row_parts)
            for k, (start, size) in enumerate(blocks[q]):
                inner = pl.ds(pl.multiple_of(p * rows + start, 128), size)
                ref = sub.at[q, inner, :]
                pltpu.make_async_copy(ref, ref, sub_recv.at[q, k, p]).wait()

                @pl.loop(0, size // deep)
                def _(i):
                    block = sub[q, piece(i, deep, p * rows + start), :].astype(jnp.float32)
                    swapped = exchange_quarters(block)
                    for n, value in enumerate((turn(block), swapped, turn(swapped))):
                        turned[n // 2, piece(i, deep, n % 2 * left), :] = value.astype(jnp.bfloat16)

                def product_sub(span):
                    columns = [sub[q, inner, :]] + [turned[n // 2, pl.ds(n % 2 * left, size), :] for n in range(3)]
                    return multiply(span, inner, columns) + total[1, span, q * lanes:(q + 1) * lanes]

                if d < row_parts - 1 or k < len(blocks[q]) - 1:
                    for i in range(rows // tall):
                        span = piece(i, tall)
                        total[1, span, q * lanes:(q + 1) * lanes] = product_sub(span)
                    continue

                for i in range(rows // slim):
                    out = product_sub(piece(i, slim))
                    here = piece(i, pair)
                    for (way, present, other), block in zip(ways, swap_quarters(out[:pair], out[pair:])):
                        ours, at = piece(i, pair, q * (rows // 2)), (2 + way) * lanes
                        stage[ours, at:at + lanes] = block.astype(jnp.bfloat16)

                        @pl.when(present)
                        def _():
                            pltpu.make_async_remote_copy(
                                src_ref=stage.at[ours, at:at + lanes],
                                dst_ref=final_sub.at[q, way, here, :],
                                send_sem=last_send.at[q, way],
                                recv_sem=last_recv.at[q, way],
                                device_id=(other, part),
                                device_id_type=MESH,
                            ).start()

    @pl.loop(0, 2 * LAST - 1)
    def _(step):
        tick, group = step // 2, step % 2
        own_half(tick, group)
        take_next(step + 1)
        other_half(tick, group)

    own_half(LAST - 1, 1)
    take_last()
    own_half(LAST, 0, False)
    other_half(LAST - 1, 1)
    pairs = [(d, k) for d in range(1, row_parts) for k in range(rows // big)]
    ahead = max(rows // big - 1, 0)
    for i in range(rows // big):
        relay(2 * LAST - 2, i, True)
    other_last(pairs[:1])
    take_sub()
    own_sub()
    other_last(pairs[1:])
    joint_sub()
    for q in range(2):
        other_sub(q)

    def whole(ref, sem):
        pltpu.make_async_copy(ref, ref, sem).wait()

    for way, came, goes in ((0, has_above, has_below), (1, has_below, has_above)):
        def sent(tick, group):
            for d in range(1, row_parts):
                whole(current.at[tick, group, way, own, :], row_send.at[tick, group, way, d - 1])

        for group in range(2):
            sent(0, group)

        @pl.when(came)
        def _():
            for step in range(2, 2 * LAST + 1):
                @pl.when(jnp.logical_not(crosses_early(step - 2, way, sender(way))))
                def _():
                    sent(step // 2, step % 2)
            if joint:
                for d in range(1, row_parts):
                    whole(current.at[LAST, 1, way, piece(0, joint, own_base), :], row_send.at[LAST, 1, way, d - 1])
            whole(final.at[way], final_sem.at[way])
            for q in range(2):
                whole(final_sub.at[q, way], last_recv.at[q, way])

        @pl.when(jnp.logical_not(came))
        def _():
            for copy in zero_final(way):
                copy.wait()

        @pl.when(goes)
        def _():
            for step in range(2 * LAST + 1):
                whole(outgoing.at[0, way], send_sem.at[step, way])
            for q in range(2):
                whole(outgoing.at[0, way, pl.ds(0, rows // 2), :], last_send.at[q, way])

        if early:
            for step in range(2 * LAST - 1):
                @pl.when(crosses_early(step, way, layer))
                def _():
                    for sem in relay_refs[1:3]:
                        whole(outgoing.at[step, way], sem.at[step])

    for q in range(2):
        for d in range(1, row_parts):
            whole(sub.at[q, piece(0, rows - joint, own_base + joint), :], sub_send.at[q, d - 1])


def unpack(chunk, slim, final, final_sub, result, first, second, natural, first_sem, second_sem, out_sem):
    rows, lanes = first.shape[1], first.shape[2]
    pair = chunk // 2
    chunks = rows // chunk

    def takes(i):
        full, half = pl.ds(i * chunk, chunk), pl.ds(i * pair, pair)
        return (
            pltpu.make_async_copy(final.at[:, full, :], first.at[:, full, :], first_sem.at[i]),
            pltpu.make_async_copy(final_sub.at[:, :, half, :], second.at[:, :, half, :], second_sem.at[i]),
        )

    def put(i):
        full = pl.ds(i * chunk, chunk)
        return pltpu.make_async_copy(natural.at[full, :], result.at[0, full, :], out_sem.at[i])

    for i in range(chunks):
        for copy in takes(i):
            copy.start()
    for i in range(chunks):
        for copy in takes(i):
            copy.wait()
        full, half = pl.ds(i * chunk, chunk), pl.ds(i * pair, pair)
        for way in range(2):
            a = first[way, full, :]
            parts = []
            for j in range(chunk // slim):
                short = pl.ds(i * pair + j * (slim // 2), slim // 2)
                parts += swap_quarters(*(second[q, way, short, :] for q in range(2)))
            b = jnp.concatenate(parts, 0)
            for n, block in enumerate(swap_halves(a, b)):
                at = (2 * way + n) * lanes
                natural[full, at:at + lanes] = block
        put(i).start()
    for i in range(chunks):
        put(i).wait()


def level(layers):
    chips = layers // 2
    counts = [(2 * i + 1, min(2 * LAST - 1, 4 - 8 * (i + 1) // chips)) for i in range(chips // 2 - 1)]
    return tuple((rank, count) for rank, count in counts if count > 0)


def per_device(waves, operators, sources, source_layer):
    layers, row_parts = lax.axis_size("layer"), lax.axis_size("row")
    rows, depth = operators.shape[2], operators.shape[3]
    lanes = waves.shape[2] // 4
    fine, chunk, big, tall, slim, deep, broad = (math.gcd(rows, size) for size in (256, 512, 512, 256, 256, 384, 512))
    deep = deep if deep < rows else math.gcd(rows, 128)
    joint = rows // deep // 2 * deep
    early = ()
    pieces, steps = rows // broad, 2 * LAST + 1
    peers = row_parts - 1
    anywhere = pl.BlockSpec(memory_space=pl.ANY)
    dma = pltpu.SemaphoreType.DMA
    relays = 2 * LAST - 1
    relay_shapes = [
        pltpu.VMEM((relays, rows, lanes), jnp.bfloat16),
        dma((relays,)),
        dma((relays,)),
        dma((relays, rows // big)),
    ] if early else []
    final, final_sub = pl.pallas_call(
        functools.partial(kernel, layers, row_parts, fine, chunk, big, tall, slim, joint, deep, early),
        out_shape=(
            jax.ShapeDtypeStruct((2, rows, lanes), jnp.bfloat16),
            jax.ShapeDtypeStruct((2, 2, rows // 2, lanes), jnp.bfloat16),
        ),
        in_specs=[anywhere, anywhere, anywhere, pl.BlockSpec(memory_space=pltpu.VMEM)],
        out_specs=(anywhere, anywhere),
        scratch_shapes=[
            pltpu.VMEM((4, rows, depth), jnp.bfloat16),
            pltpu.VMEM((TICKS, 2, 2, depth, lanes), jnp.bfloat16),
            pltpu.VMEM((2, max(rows, 2 * (rows - joint)), lanes), jnp.bfloat16),
            pltpu.VMEM((2, rows, 2 * lanes), jnp.float32),
            pltpu.VMEM((steps - 1, 2, rows, lanes), jnp.bfloat16),
            pltpu.VMEM((2, 2, rows, lanes), jnp.bfloat16),
            pltpu.VMEM((rows, 4 * lanes), jnp.bfloat16),
            pltpu.VMEM((2, depth, lanes), jnp.bfloat16),
            dma((rows // fine,)),
            dma((1,)),
            dma((rows // big,)),
            dma((2, 3)),
            dma((TICKS, 2, 2, peers)),
            dma((steps, 2)),
            dma((TICKS, 2, 2, row_parts)),
            dma((2,)),
            dma((2, rows // big, row_parts)),
            dma((2, peers)),
            dma((2, (rows - joint) // deep, row_parts)),
            dma((2, 2)),
            dma((2, 2)),
            *relay_shapes,
        ],
        compiler_params=pltpu.CompilerParams(
            collective_id=0, has_side_effects=True, vmem_limit_bytes=67043328
        ),
    )(waves, operators, sources, source_layer.reshape(1, lanes))
    return pl.pallas_call(
        functools.partial(unpack, broad, slim),
        out_shape=jax.ShapeDtypeStruct(waves.shape, jnp.bfloat16),
        in_specs=[anywhere, anywhere],
        out_specs=anywhere,
        scratch_shapes=[
            pltpu.VMEM(final.shape, jnp.bfloat16),
            pltpu.VMEM(final_sub.shape, jnp.bfloat16),
            pltpu.VMEM((rows, 4 * lanes), jnp.bfloat16),
            dma((pieces,)),
            dma((pieces,)),
            dma((pieces,)),
        ],
    )(final, final_sub)


def solution(mesh):
    return jax.shard_map(
        per_device,
        mesh=mesh,
        in_specs=(P("layer", "row", None), P("layer", None, "row", None), P("row", None), P()),
        out_specs=P("layer", "row", None),
        check_vma=False,
    )
```
